256 devices in a mesh: group: 16 (over x, z_hi, core), blk: 16 (over y, z_lo).
Axes of the slice: x: 4, y: 4, z: 8 (z_hi: 2, z_lo: 4; z = z_hi * 4 + z_lo), core: 2. Of those that a mesh axis runs over, the one named last changes fastest.
Arguments:
- tokens: bfloat16 [12288, 7168], P(('group', 'blk')), may hold values from -6 to 6
- cotangent: bfloat16 [12288, 7168], P(('group', 'blk')), may hold values from -6 to 6
- w_gate: bfloat16 [16, 7168, 2048], P('group', None, 'blk'), may hold values from -0.0625 to 0.0625
- w_up: bfloat16 [16, 7168, 2048], P('group', None, 'blk'), may hold values from -0.0625 to 0.0625
- w_down: bfloat16 [16, 2048, 7168], P('group', 'blk'), may hold values from -0.125 to 0.125
- gate_weight: float32 [256, 16, 2], P(('group', 'blk')), may hold values from 0.1 to 1
- counts: int32 [256, 16], P(('group', 'blk')), may hold values from 0 to 2, as said below
- slots: int32 [256, 16, 2], P(('group', 'blk')), may hold values from 0 to 47, as said below
Outputs:
- grad_tokens: bfloat16 [12288, 7168], P(('group', 'blk'))
- grad_gate: bfloat16 [16, 7168, 2048], P('group', None, 'blk')
- grad_up: bfloat16 [16, 7168, 2048], P('group', None, 'blk')
- grad_down: bfloat16 [16, 2048, 7168], P('group', 'blk')
The draws below stay inside these ranges and needn't reach their ends.
Inputs may be any that keep to these rules, and one draw needn't show every extreme that they name: `counts`: in every draw one expert has 2 tokens from every device. `slots`: the 2 entries of one device's list for one expert are different tokens.
All inputs are finite; a program needn't handle non-finite values.
Results may differ from the reference program's by a relative error of at most 0.018.
Values may be sent and summed in bfloat16 or wider, within the bound.
A program may use at most 128 MiB of HBM per device.

```python
import jax
import jax.numpy as jnp
from jax import lax

D = 7168
HID = 2048
TOK_DEV = 48
CAP = 2
EXPERTS = 16
SOURCES = 256
TOKENS = 12288
N_BLK = 16


def draw_counts(key, part):
    key_base, key_full = jax.random.split(key)
    base = jax.random.randint(key_base, (SOURCES, EXPERTS), 0, CAP + 1)
    full_expert = jax.random.randint(key_full, (), 0, EXPERTS)
    column = lax.broadcasted_iota(jnp.int32, (SOURCES, EXPERTS), 1)
    return jnp.where(column == full_expert, CAP, base).astype(jnp.int32)


def draw_slots(key, part):
    keys = jax.random.split(key, SOURCES * EXPERTS)

    def one_list(single_key):
        return jax.random.permutation(single_key, TOK_DEV)[:CAP]
    lists = jax.vmap(one_list)(keys)
    return lists.reshape(SOURCES, EXPERTS, CAP).astype(jnp.int32)


def shard_levels(stream_key, shape, pieces, least, top_value):
    factor_of, own = 1.0, jax.random.fold_in(stream_key, 6)
    for dim, shards_of in pieces:
        heights = jnp.exp(jax.random.uniform(jax.random.fold_in(own, dim), (shards_of,), jnp.float32, least / len(pieces), top_value / len(pieces)))
        factor_of = factor_of * jnp.repeat(heights, shape[dim] // shards_of).reshape([-1 if axis == dim else 1 for axis in range(len(shape))])
    return factor_of


def centred(rng, dims, deviation, most, cuts=(), dtype=jnp.bfloat16):
    entries = deviation * jax.random.normal(rng, dims, jnp.float32)
    if cuts:
        entries = entries * shard_levels(rng, dims, cuts, -0.22, 0.18)
    return jnp.clip(entries, -most, most).astype(dtype)


def setup_inputs(seed: int = 0) -> dict:
    streams_of = jax.random.split(jax.random.key(seed), 9)
    return {
        "tokens": centred(streams_of[0], (TOKENS, D), 1.0, 6.0, ((0, 256),)),
        "cotangent": centred(streams_of[1], (TOKENS, D), 1.0, 6.0, ((0, 256),)),
        "w_gate": centred(streams_of[2], (EXPERTS, D, HID), D ** -0.5, 0.0625, ((0, 16), (2, 16))),
        "w_up": centred(streams_of[3], (EXPERTS, D, HID), D ** -0.5, 0.0625, ((0, 16), (2, 16))),
        "w_down": centred(streams_of[4], (EXPERTS, HID, D), HID ** -0.5, 0.125, ((0, 16), (1, 16))),
        "gate_weight": jnp.clip(0.1 + 0.9 * jax.random.uniform(streams_of[5], (SOURCES, EXPERTS, CAP), jnp.float32) ** shard_levels(streams_of[5], (SOURCES, EXPERTS, CAP), ((0, 256),), -0.2, 0.2), 0.1, 1.0),
        "counts": draw_counts(jax.random.fold_in(streams_of[8], 71), 0),
        "slots": draw_slots(jax.random.fold_in(streams_of[8], 71), 0),
    }


def reference(tokens, cotangent, w_gate, w_up, w_down, gate_weight, counts, slots):
    position = lax.broadcasted_iota(jnp.int32, (SOURCES, EXPERTS, CAP), 2)
    live = jnp.where(position < counts[:, :, None], gate_weight, jnp.zeros_like(gate_weight))
    source_row = lax.broadcasted_iota(jnp.int32, (SOURCES, EXPERTS, CAP), 0) * TOK_DEV
    token_index = (source_row + slots).astype(jnp.int32)
    block_width = HID // N_BLK

    def per_expert(grad_sum, inputs):
        index, weight, gate_mat, up_mat, down_mat = inputs
        flat = index.reshape(-1).astype(jnp.int32)
        rows_in = jnp.take(tokens, flat, axis=0)
        scaled = (weight.reshape(-1, 1) * jnp.take(cotangent, flat, axis=0).astype(jnp.float32)).astype(jnp.bfloat16)
        pre_gate = jnp.dot(rows_in, gate_mat, preferred_element_type=jnp.float32)
        pre_up = jnp.dot(rows_in, up_mat, preferred_element_type=jnp.float32)
        sigma = jax.nn.sigmoid(pre_gate)
        silu_val = pre_gate * sigma
        act = (silu_val * pre_up).astype(jnp.bfloat16)
        grad_hidden = jnp.dot(scaled, down_mat.T, preferred_element_type=jnp.float32)
        grad_pre_gate = (grad_hidden * pre_up * sigma * (1.0 + pre_gate * (1.0 - sigma))).astype(jnp.bfloat16)
        grad_pre_up = (grad_hidden * silu_val).astype(jnp.bfloat16)
        grad_down = jnp.dot(act.T, scaled, preferred_element_type=jnp.float32).astype(jnp.bfloat16)
        grad_gate = jnp.dot(rows_in.T, grad_pre_gate, preferred_element_type=jnp.float32).astype(jnp.bfloat16)
        grad_up = jnp.dot(rows_in.T, grad_pre_up, preferred_element_type=jnp.float32).astype(jnp.bfloat16)
        slot_grad = jnp.zeros((flat.shape[0], D), jnp.float32)
        for block in range(N_BLK):
            lower = block * block_width
            upper = lower + block_width
            part = jnp.dot(grad_pre_gate[:, lower:upper], gate_mat[:, lower:upper].T, preferred_element_type=jnp.float32)
            part = part + jnp.dot(grad_pre_up[:, lower:upper], up_mat[:, lower:upper].T, preferred_element_type=jnp.float32)
            rounded = lax.optimization_barrier(part.astype(jnp.bfloat16))
            slot_grad = slot_grad + rounded.astype(jnp.float32)
        grad_sum = grad_sum.at[flat].add(slot_grad)
        return grad_sum, (grad_gate, grad_up, grad_down)

    start = jnp.zeros((TOKENS, D), jnp.float32)
    inputs = (jnp.transpose(token_index, (1, 0, 2)), jnp.transpose(live, (1, 0, 2)), w_gate, w_up, w_down)
    grad_sum, grads = lax.scan(per_expert, start, inputs)
    return grad_sum.astype(jnp.bfloat16), grads[0], grads[1], grads[2]
```

```python
import functools

import jax
import jax.numpy as jnp
from jax import lax
from jax.experimental import pallas as pl
from jax.experimental.pallas import tpu as pltpu
from jax.sharding import PartitionSpec as P

MESH = pl.DeviceIdType.MESH
NX, NY, NZ, NC, RUN = 4, 4, 8, 2, 4
Q = 4
HOPS = (0, 1, 7, 2, 6, 3, 5, 4)


def contract_rows(left, right):
    return lax.dot_general(
        left, right, (((0,), (0,)), ((), ())), preferred_element_type=jnp.float32
    )


def contract_cols(left, right):
    return lax.dot_general(
        left, right, (((1,), (1,)), ((), ())), preferred_element_type=jnp.float32
    )


def place():
    group, blk = lax.axis_index("group"), lax.axis_index("blk")
    x, z_hi, core = group // 4, (group // 2) % 2, group % 2
    y, z_lo = blk // RUN, blk % RUN
    return x, y, z_hi * RUN + z_lo, core


def device(x, y, z, core):
    return (x * 4 + (z // RUN) * 2 + core, y * RUN + z % RUN)


def x_peers(me):
    x, y, z, core = me
    for step in range(1, NX * NC):
        px, pc = (x + step // NC) % NX, (core + step % NC) % NC
        yield step - 1, px * NC + pc, device(px, y, z, pc)


def greet(me):
    x, y, z, core = me
    barrier = pltpu.get_barrier_semaphore()
    peers = [d for _, _, d in x_peers(me)]
    peers += [device(x, y, (z + hop) % NZ, core) for hop in range(1, NZ)]
    peers += [device(x, (y + 1) % NY, z, core), device(x, (y + 3) % NY, z, core)]
    for peer in peers:
        pl.semaphore_signal(barrier, inc=1, device_id=peer, device_id_type=MESH)
    pl.semaphore_wait(barrier, len(peers))


def remote(src, dst, send, recv, to):
    return pltpu.make_async_remote_copy(
        src_ref=src, dst_ref=dst, send_sem=send, recv_sem=recv, device_id=to, device_id_type=MESH
    )


def order_matrix():
    row = lax.broadcasted_iota(jnp.int32, (128, 128), 0)
    col = lax.broadcasted_iota(jnp.int32, (128, 128), 1)
    h, q, s, c = row // 64, (row // 16) % 4, (row // 2) % 8, row % 2
    return (col == s * 16 + h * 8 + c * 4 + q).astype(jnp.bfloat16)


def spread_kernel(
    tok_ref, cot_ref, pick_ref, scale_ref, out_in, out_sc,
    mess, recv, block, xs, xr, zs, zr, ys, yr, fs, fr, own_sem,
):
    me = place()
    x, y, z, core = me
    mine = x * NC + core
    width = tok_ref.shape[1] // Q
    half = tok_ref.shape[1] // 2
    outs = (out_in, out_sc)
    order = order_matrix()
    up, down = device(x, (y + 1) % NY, z, core), device(x, (y + 3) % NY, z, core)
    greet(me)

    def x_copy(t, i, slot, to):
        return remote(mess.at[t, slot], recv.at[t, mine], xs.at[t, i], xr.at[t, i], to)

    for t, rows_ref in enumerate((tok_ref, cot_ref)):
        total = jnp.zeros((128, width), jnp.float32)
        for q in range(Q):
            total = total + jnp.dot(
                pick_ref[q], rows_ref[:, q * width:(q + 1) * width],
                preferred_element_type=jnp.float32,
            )
        if t == 1:
            total = total * scale_ref[...]
        mess[t] = total.astype(jnp.bfloat16).reshape(8, 16, width)
        for i, slot, to in x_peers(me):
            x_copy(t, i, slot, to).start()
        recv[t, pl.ds(mine, 1)] = mess[t, pl.ds(mine, 1)]

    def z_copy(t, k):
        zt = (z + HOPS[k]) % NZ
        return remote(
            block.at[t, zt // RUN], outs[t].at[0, k], zs.at[t, k], zr.at[t, k],
            device(x, y, zt, core),
        )

    def y_copy(t, k, side, src=None):
        src = outs[t].at[0, k] if src is None else src
        return remote(
            src, outs[t].at[1 + side, k], ys.at[t, side, k], yr.at[t, side, k],
            down if side else up,
        )

    def f_copy(t, k, side):
        cols = pl.ds(side * half, half)
        return remote(
            outs[t].at[1 + side, k, :, cols], outs[t].at[3, k, :, cols],
            fs.at[t, side, k], fr.at[t, side, k], down if side else up,
        )

    def own_copy(t):
        return pltpu.make_async_copy(block.at[t, z // RUN], outs[t].at[0, 0], own_sem.at[t])

    for t in range(2):
        for i, slot, to in x_peers(me):
            x_copy(t, i, slot, to).wait_recv()
        rows = jnp.dot(
            order, recv[t].reshape(128, width), preferred_element_type=jnp.float32
        ).astype(jnp.bfloat16)
        for h in range(2):
            for q in range(Q):
                start = (h * Q + q) * 16
                block[t, h, :, q * width:(q + 1) * width] = rows[start:start + 16]
        for side in range(2):
            y_copy(t, 0, side, block.at[t, z // RUN]).start()
        for k in range(1, NZ):
            z_copy(t, k).start()
        own_copy(t).start()

    def forward(t, k):
        for side in range(2):
            y_copy(t, k, side).wait_recv()
            f_copy(t, k, side).start()

    for t in range(2):
        @pl.loop(1, NZ)
        def _(k, t=t):
            zt = z
            remote(
                block.at[t, 0], outs[t].at[0, k], zs.at[t, k], zr.at[t, k], (up[0], up[1])
            ).wait_recv()
            for side in range(2):
                y_copy(t, k, side).start()
            forward(t, k - 1)

    for t in range(2):
        forward(t, NZ - 1)
    for t in range(2):
        own_copy(t).wait()
        for i, slot, to in x_peers(me):
            x_copy(t, i, slot, to).wait_send()

        @pl.loop(0, NZ)
        def _(k, t=t):
            for side in range(2):
                y_copy(t, k, side).wait_send()
                f_copy(t, k, side).wait()

        for k in range(1, NZ):
            z_copy(t, k).wait_send()


def spread(tokens, cotangent, pick, scale):
    dim = tokens.shape[1]
    out = jax.ShapeDtypeStruct((4, NZ, 16, dim), jnp.bfloat16)
    vmem = pl.BlockSpec(memory_space=pltpu.VMEM)
    dma = pltpu.SemaphoreType.DMA
    return pl.pallas_call(
        spread_kernel,
        out_shape=(out, out),
        in_specs=[vmem] * 4,
        out_specs=(pl.BlockSpec(memory_space=pl.ANY),) * 2,
        scratch_shapes=[
            pltpu.VMEM((2, 8, 16, dim // Q), jnp.bfloat16),
            pltpu.VMEM((2, 8, 16, dim // Q), jnp.bfloat16),
            pltpu.VMEM((2, 2, 16, dim), jnp.bfloat16),
            dma((2, 7)), dma((2, 7)), dma((2, NZ)), dma((2, NZ)),
            dma((2, 2, NZ)), dma((2, 2, NZ)), dma((2, 2, NZ)), dma((2, 2, NZ)), dma((2,)),
        ],
        compiler_params=pltpu.CompilerParams(
            collective_id=0, has_side_effects=True, vmem_limit_bytes=40 * 2**20
        ),
        name="spread",
    )(tokens, cotangent, pick, scale)


def collect_kernel(
    part, pick_ref, out_ref,
    half_in, stage, side_in, summed, z_in, mess, recv,
    hs, hr, ds, dr, ss, sr, zs, zr, xs, xr,
):
    me = place()
    x, y, z, core = me
    mine = x * NC + core
    dim = part.shape[-1]
    width, half = dim // Q, dim // 2
    order = order_matrix()
    up, down = device(x, (y + 1) % NY, z, core), device(x, (y + 3) % NY, z, core)
    greet(me)
    cols = (pl.ds(0, half), pl.ds(half, half))
    sides = (down, up)

    def h_copy(k, side):
        return remote(
            part.at[3, k, :, cols[side]], half_in.at[side, k],
            hs.at[side, k], hr.at[side, k], sides[side],
        )

    def d_copy(k, side):
        return remote(
            part.at[1 + side, k, :, cols[1 - side]], side_in.at[side, k, :, cols[1 - side]],
            ds.at[side, k], dr.at[side, k], sides[side],
        )

    def s_copy(k, side):
        return remote(
            stage.at[side, k], side_in.at[side, k, :, cols[side]],
            ss.at[side, k], sr.at[side, k], sides[side],
        )

    def z_copy(k):
        zt = (z + NZ - HOPS[k]) % NZ
        return remote(
            summed.at[k], z_in.at[z], zs.at[k], zr.at[k], device(x, y, zt, core)
        )

    @pl.loop(0, NZ)
    def _(k):
        for side in range(2):
            h_copy(k, side).start()
            d_copy(k, side).start()

    f32 = jnp.float32

    def relay(k):
        for side in range(2):
            h_copy(k, side).wait_recv()
            stage[side, k] = (
                half_in[side, k].astype(f32) + part[1 + side, k, :, cols[side]].astype(f32)
            ).astype(jnp.bfloat16)
            s_copy(k, side).start()

    def total(k):
        for side in range(2):
            d_copy(k, side).wait_recv()
            s_copy(k, side).wait_recv()
        return (
            part[0, k].astype(f32) + side_in[0, k].astype(f32) + side_in[1, k].astype(f32)
        ).astype(jnp.bfloat16)

    relay(0)
    for k in range(NZ):
        if k + 1 < NZ:
            relay(k + 1)
        if k == 0:
            z_in[pl.ds(z, 1)] = total(k)[None]
        else:
            summed[k] = total(k)
            z_copy(k).start()

    for k in range(1, NZ):
        z_copy(k).wait_recv()
    pieces = []
    for h in range(2):
        for q in range(Q):
            c = slice(q * width, (q + 1) * width)
            acc = z_in[h * RUN, :, c].astype(f32)
            for l in range(1, RUN):
                acc = acc + z_in[h * RUN + l, :, c].astype(f32)
            pieces.append(acc.astype(jnp.bfloat16))
    mess[...] = contract_rows(order, jnp.concatenate(pieces, axis=0)).astype(
        jnp.bfloat16
    ).reshape(8, 16, width)

    def x_copy(i, slot, to):
        return remote(mess.at[slot], recv.at[mine], xs.at[i], xr.at[i], to)

    for i, slot, to in x_peers(me):
        x_copy(i, slot, to).start()
    recv[pl.ds(mine, 1)] = mess[pl.ds(mine, 1)]
    for i, slot, to in x_peers(me):
        x_copy(i, slot, to).wait_recv()
    for q in range(Q):
        out_ref[:, q * width:(q + 1) * width] = contract_rows(
            pick_ref[q], recv[...].reshape(128, width)
        ).astype(jnp.bfloat16)

    for i, slot, to in x_peers(me):
        x_copy(i, slot, to).wait_send()

    @pl.loop(0, NZ)
    def _(k):
        for side in range(2):
            h_copy(k, side).wait_send()
            d_copy(k, side).wait_send()
            s_copy(k, side).wait_send()

    for k in range(1, NZ):
        z_copy(k).wait_send()


def collect(part, pick, tok_dev):
    dim = part.shape[-1]
    vmem = pl.BlockSpec(memory_space=pltpu.VMEM)
    dma = pltpu.SemaphoreType.DMA
    bf = jnp.bfloat16
    pair = dma((2, NZ))
    return pl.pallas_call(
        collect_kernel,
        out_shape=jax.ShapeDtypeStruct((tok_dev, dim), bf),
        in_specs=[vmem] * 2,
        out_specs=vmem,
        scratch_shapes=[
            pltpu.VMEM((2, NZ, 16, dim // 2), bf),
            pltpu.VMEM((2, NZ, 16, dim // 2), bf),
            pltpu.VMEM((2, NZ, 16, dim), bf),
            pltpu.VMEM((NZ, 16, dim), bf),
            pltpu.VMEM((NZ, 16, dim), bf),
            pltpu.VMEM((8, 16, dim // Q), bf),
            pltpu.VMEM((8, 16, dim // Q), bf),
            pair, pair, pair, pair, pair, pair,
            dma((NZ,)), dma((NZ,)), dma((7,)), dma((7,)),
        ],
        compiler_params=pltpu.CompilerParams(
            collective_id=1, has_side_effects=True, vmem_limit_bytes=48 * 2**20
        ),
        name="collect",
    )(part, pick)


def body(tokens, cotangent, w_gate, w_up, w_down, gate_weight, counts, slots):
    experts = counts.shape[1]
    cap = slots.shape[2]
    tok_dev = tokens.shape[0]
    width = tokens.shape[1]
    position = lax.broadcasted_iota(jnp.int32, (experts, cap), 1)
    live = jnp.where(position < counts[0][:, None], gate_weight[0], jnp.zeros_like(gate_weight[0]))

    def rows(a):
        a = a.reshape(NX, 2, NC, cap).transpose(0, 2, 1, 3).reshape(experts * cap, 1)
        return jnp.broadcast_to(a, (experts * cap, Q)).reshape(experts * cap * Q, 1)

    slot_rows = rows(slots[0])
    dims = (Q, experts * cap * Q, tok_dev)
    pick = (
        (slot_rows[None] == lax.broadcasted_iota(jnp.int32, dims, 2))
        & (lax.broadcasted_iota(jnp.int32, dims, 1) % Q == lax.broadcasted_iota(jnp.int32, dims, 0))
    ).astype(jnp.bfloat16)
    got_in, got_scaled = spread(tokens, cotangent, pick, rows(live))
    flat_in = got_in.reshape(-1, width)
    flat_scaled = got_scaled.reshape(-1, width)
    gate_mat, up_mat, down_mat = w_gate[0], w_up[0], w_down[0]
    pre_gate = jnp.dot(flat_in, gate_mat, preferred_element_type=jnp.float32)
    pre_up = jnp.dot(flat_in, up_mat, preferred_element_type=jnp.float32)
    sigma = jax.nn.sigmoid(pre_gate)
    silu_val = pre_gate * sigma
    act = (silu_val * pre_up).astype(jnp.bfloat16)
    grad_hidden = contract_cols(flat_scaled, down_mat)
    grad_pre_gate = (grad_hidden * pre_up * sigma * (1.0 + pre_gate * (1.0 - sigma))).astype(
        jnp.bfloat16
    )
    grad_pre_up = (grad_hidden * silu_val).astype(jnp.bfloat16)
    acc_gate = contract_rows(flat_in, grad_pre_gate)
    acc_up = contract_rows(flat_in, grad_pre_up)
    acc_down = contract_rows(act, flat_scaled)
    part = contract_cols(grad_pre_gate, gate_mat) + contract_cols(grad_pre_up, up_mat)
    part = part.astype(jnp.bfloat16).reshape(4, NZ, 16, width)
    grad_tokens = collect(part, pick, tok_dev)
    return (
        grad_tokens,
        acc_gate.astype(jnp.bfloat16)[None],
        acc_up.astype(jnp.bfloat16)[None],
        acc_down.astype(jnp.bfloat16)[None],
    )


def solution(mesh):
    in_specs = (
        P(("group", "blk"), None),
        P(("group", "blk"), None),
        P("group", None, "blk"),
        P("group", None, "blk"),
        P("group", "blk", None),
        P(("group", "blk"), None, None),
        P(("group", "blk"), None),
        P(("group", "blk"), None, None),
    )
    out_specs = (
        P(("group", "blk"), None),
        P("group", None, "blk"),
        P("group", None, "blk"),
        P("group", "blk", None),
    )
    return jax.shard_map(body, mesh=mesh, in_specs=in_specs, out_specs=out_specs, check_vma=False)
```

```python
import functools

import jax
import jax.numpy as jnp
from jax import lax
from jax.experimental import pallas as pl
from jax.experimental.pallas import tpu as pltpu
from jax.sharding import PartitionSpec as P

MESH = pl.DeviceIdType.MESH
NX, NY, NZ, NC, RUN = 4, 4, 8, 2, 4
Q = 4
HOPS = (0, 1, 7, 2, 6, 3, 5, 4)


def contract_rows(left, right):
    return lax.dot_general(
        left, right, (((0,), (0,)), ((), ())), preferred_element_type=jnp.float32
    )


def contract_cols(left, right):
    return lax.dot_general(
        left, right, (((1,), (1,)), ((), ())), preferred_element_type=jnp.float32
    )


def place():
    group, blk = lax.axis_index("group"), lax.axis_index("blk")
    x, z_hi, core = group // 4, (group // 2) % 2, group % 2
    y, z_lo = blk // RUN, blk % RUN
    return x, y, z_hi * RUN + z_lo, core


def device(x, y, z, core):
    return (x * 4 + (z // RUN) * 2 + core, y * RUN + z % RUN)


def x_peers(me):
    x, y, z, core = me
    for step in range(1, NX * NC):
        px, pc = (x + step // NC) % NX, (core + step % NC) % NC
        yield step - 1, px * NC + pc, device(px, y, z, pc)


def greet(me):
    x, y, z, core = me
    barrier = pltpu.get_barrier_semaphore()
    peers = [d for _, _, d in x_peers(me)]
    peers += [device(x, y, (z + hop) % NZ, core) for hop in range(1, NZ)]
    peers += [device(x, (y + 1) % NY, z, core), device(x, (y + 3) % NY, z, core)]
    for peer in peers:
        pl.semaphore_signal(barrier, inc=1, device_id=peer, device_id_type=MESH)
    pl.semaphore_wait(barrier, len(peers))


def remote(src, dst, send, recv, to):
    return pltpu.make_async_remote_copy(
        src_ref=src, dst_ref=dst, send_sem=send, recv_sem=recv, device_id=to, device_id_type=MESH
    )


def order_matrix():
    row = lax.broadcasted_iota(jnp.int32, (128, 128), 0)
    col = lax.broadcasted_iota(jnp.int32, (128, 128), 1)
    h, q, s, c = row // 64, (row // 16) % 4, (row // 2) % 8, row % 2
    return (col == s * 16 + h * 8 + c * 4 + q).astype(jnp.bfloat16)


def spread_kernel(
    tok_ref, cot_ref, pick_ref, scale_ref, out_in, out_sc,
    mess, recv, block, xs, xr, zs, zr, ys, yr, fs, fr, own_sem,
):
    me = place()
    x, y, z, core = me
    mine = x * NC + core
    width = tok_ref.shape[1] // Q
    half = tok_ref.shape[1] // 2
    outs = (out_in, out_sc)
    order = order_matrix()
    up, down = device(x, (y + 1) % NY, z, core), device(x, (y + 3) % NY, z, core)
    greet(me)

    def x_copy(t, i, slot, to):
        return remote(mess.at[t, slot], recv.at[t, mine], xs.at[t, i], xr.at[t, i], to)

    for t, rows_ref in enumerate((tok_ref, cot_ref)):
        total = jnp.zeros((128, width), jnp.float32)
        for q in range(Q):
            total = total + jnp.dot(
                pick_ref[q], rows_ref[:, q * width:(q + 1) * width],
                preferred_element_type=jnp.float32,
            )
        if t == 1:
            total = total * scale_ref[...]
        mess[t] = total.astype(jnp.bfloat16).reshape(8, 16, width)
        for i, slot, to in x_peers(me):
            x_copy(t, i, slot, to).start()
        recv[t, pl.ds(mine, 1)] = mess[t, pl.ds(mine, 1)]

    def z_copy(t, k):
        zt = (z + HOPS[k]) % NZ
        return remote(
            block.at[t, zt // RUN], outs[t].at[0, k], zs.at[t, k], zr.at[t, k],
            device(x, y, zt, core),
        )

    def y_copy(t, k, side, src=None):
        src = outs[t].at[0, k] if src is None else src
        return remote(
            src, outs[t].at[1 + side, k], ys.at[t, side, k], yr.at[t, side, k],
            down if side else up,
        )

    def f_copy(t, k, side):
        cols = pl.ds(side * half, half)
        return remote(
            outs[t].at[1 + side, k, :, cols], outs[t].at[3, k, :, cols],
            fs.at[t, side, k], fr.at[t, side, k], down if side else up,
        )

    def own_copy(t):
        return pltpu.make_async_copy(block.at[t, z // RUN], outs[t].at[0, 0], own_sem.at[t])

    for t in range(2):
        for i, slot, to in x_peers(me):
            x_copy(t, i, slot, to).wait_recv()
        rows = jnp.dot(
            order, recv[t].reshape(128, width), preferred_element_type=jnp.float32
        ).astype(jnp.bfloat16)
        for h in range(2):
            for q in range(Q):
                start = (h * Q + q) * 16
                block[t, h, :, q * width:(q + 1) * width] = rows[start:start + 16]
        for side in range(2):
            y_copy(t, 0, side, block.at[t, z // RUN]).start()
        for k in range(1, NZ):
            z_copy(t, k).start()
        own_copy(t).start()

    def forward(t, k):
        for side in range(2):
            y_copy(t, k, side).wait_recv()
            f_copy(t, k, side).start()

    for t in range(2):
        @pl.loop(1, NZ)
        def _(k, t=t):
            remote(block.at[t, 0], outs[t].at[0, k], zs.at[t, k], zr.at[t, k], up).wait_recv()
            for side in range(2):
                y_copy(t, k, side).start()
            forward(t, k - 1)

    for t in range(2):
        forward(t, NZ - 1)
    for t in range(2):
        own_copy(t).wait()
        for i, slot, to in x_peers(me):
            x_copy(t, i, slot, to).wait_send()

        @pl.loop(0, NZ)
        def _(k, t=t):
            for side in range(2):
                y_copy(t, k, side).wait_send()
                f_copy(t, k, side).wait()

        for k in range(1, NZ):
            z_copy(t, k).wait_send()


def spread(tokens, cotangent, pick, scale):
    dim = tokens.shape[1]
    out = jax.ShapeDtypeStruct((4, NZ, 16, dim), jnp.bfloat16)
    vmem = pl.BlockSpec(memory_space=pltpu.VMEM)
    dma = pltpu.SemaphoreType.DMA
    return pl.pallas_call(
        spread_kernel,
        out_shape=(out, out),
        in_specs=[vmem] * 4,
        out_specs=(pl.BlockSpec(memory_space=pl.ANY),) * 2,
        scratch_shapes=[
            pltpu.VMEM((2, 8, 16, dim // Q), jnp.bfloat16),
            pltpu.VMEM((2, 8, 16, dim // Q), jnp.bfloat16),
            pltpu.VMEM((2, 2, 16, dim), jnp.bfloat16),
            dma((2, 7)), dma((2, 7)), dma((2, NZ)), dma((2, NZ)),
            dma((2, 2, NZ)), dma((2, 2, NZ)), dma((2, 2, NZ)), dma((2, 2, NZ)), dma((2,)),
        ],
        compiler_params=pltpu.CompilerParams(
            collective_id=0, has_side_effects=True, vmem_limit_bytes=40 * 2**20
        ),
        name="spread",
    )(tokens, cotangent, pick, scale)


def collect_kernel(
    part, pick_ref, out_ref,
    half_in, stage, side_in, summed, z_in, mess, recv,
    hs, hr, ds, dr, ss, sr, zs, zr, xs, xr,
):
    me = place()
    x, y, z, core = me
    mine = x * NC + core
    dim = part.shape[-1]
    width, half = dim // Q, dim // 2
    order = order_matrix()
    up, down = device(x, (y + 1) % NY, z, core), device(x, (y + 3) % NY, z, core)
    greet(me)
    cols = (pl.ds(0, half), pl.ds(half, half))
    sides = (down, up)

    def h_copy(k, side):
        return remote(
            part.at[3, k, :, cols[side]], half_in.at[side, k],
            hs.at[side, k], hr.at[side, k], sides[side],
        )

    def d_copy(k, side):
        return remote(
            part.at[1 + side, k, :, cols[1 - side]], side_in.at[side, k, :, cols[1 - side]],
            ds.at[side, k], dr.at[side, k], sides[side],
        )

    def s_copy(k, side):
        return remote(
            stage.at[side, k], side_in.at[side, k, :, cols[side]],
            ss.at[side, k], sr.at[side, k], sides[side],
        )

    def z_copy(k):
        zt = (z + NZ - HOPS[k]) % NZ
        return remote(
            summed.at[k], z_in.at[z], zs.at[k], zr.at[k], device(x, y, zt, core)
        )

    f32 = jnp.float32

    def first(k):
        for side in range(2):
            h_copy(k, side).start()

    def relay(k):
        for side in range(2):
            d_copy(k, side).start()
        for side in range(2):
            h_copy(k, side).wait_recv()
            stage[side, k] = (
                half_in[side, k].astype(f32) + part[1 + side, k, :, cols[side]].astype(f32)
            ).astype(jnp.bfloat16)
            s_copy(k, side).start()

    def total(k):
        for side in range(2):
            d_copy(k, side).wait_recv()
            s_copy(k, side).wait_recv()
        return (
            part[0, k].astype(f32) + side_in[0, k].astype(f32) + side_in[1, k].astype(f32)
        ).astype(jnp.bfloat16)

    for k in (7, 6, 5):
        first(k)
    relay(7)
    for k in range(NZ - 1, -1, -1):
        if k >= 3:
            first(k - 3)
        if k > 0:
            relay(k - 1)
            summed[k] = total(k)
            z_copy(k).start()
        else:
            z_in[pl.ds(z, 1)] = total(k)[None]

    for k in range(1, NZ):
        z_copy(k).wait_recv()
    pieces = []
    for h in range(2):
        for q in range(Q):
            c = slice(q * width, (q + 1) * width)
            acc = z_in[h * RUN, :, c].astype(f32)
            for l in range(1, RUN):
                acc = acc + z_in[h * RUN + l, :, c].astype(f32)
            pieces.append(acc.astype(jnp.bfloat16))
    mess[...] = contract_rows(order, jnp.concatenate(pieces, axis=0)).astype(
        jnp.bfloat16
    ).reshape(8, 16, width)

    def x_copy(i, slot, to):
        return remote(mess.at[slot], recv.at[mine], xs.at[i], xr.at[i], to)

    for i, slot, to in x_peers(me):
        x_copy(i, slot, to).start()
    recv[pl.ds(mine, 1)] = mess[pl.ds(mine, 1)]
    for i, slot, to in x_peers(me):
        x_copy(i, slot, to).wait_recv()
    for q in range(Q):
        out_ref[:, q * width:(q + 1) * width] = contract_rows(
            pick_ref[q], recv[...].reshape(128, width)
        ).astype(jnp.bfloat16)

    for i, slot, to in x_peers(me):
        x_copy(i, slot, to).wait_send()

    @pl.loop(0, NZ)
    def _(k):
        for side in range(2):
            h_copy(k, side).wait_send()
            d_copy(k, side).wait_send()
            s_copy(k, side).wait_send()

    for k in range(1, NZ):
        z_copy(k).wait_send()


def collect(part, pick, tok_dev):
    dim = part.shape[-1]
    vmem = pl.BlockSpec(memory_space=pltpu.VMEM)
    dma = pltpu.SemaphoreType.DMA
    bf = jnp.bfloat16
    pair = dma((2, NZ))
    return pl.pallas_call(
        collect_kernel,
        out_shape=jax.ShapeDtypeStruct((tok_dev, dim), bf),
        in_specs=[vmem] * 2,
        out_specs=vmem,
        scratch_shapes=[
            pltpu.VMEM((2, NZ, 16, dim // 2), bf),
            pltpu.VMEM((2, NZ, 16, dim // 2), bf),
            pltpu.VMEM((2, NZ, 16, dim), bf),
            pltpu.VMEM((NZ, 16, dim), bf),
            pltpu.VMEM((NZ, 16, dim), bf),
            pltpu.VMEM((8, 16, dim // Q), bf),
            pltpu.VMEM((8, 16, dim // Q), bf),
            pair, pair, pair, pair, pair, pair,
            dma((NZ,)), dma((NZ,)), dma((7,)), dma((7,)),
        ],
        compiler_params=pltpu.CompilerParams(
            collective_id=1, has_side_effects=True, vmem_limit_bytes=48 * 2**20
        ),
        name="collect",
    )(part, pick)


def body(tokens, cotangent, w_gate, w_up, w_down, gate_weight, counts, slots):
    experts = counts.shape[1]
    cap = slots.shape[2]
    tok_dev = tokens.shape[0]
    width = tokens.shape[1]
    position = lax.broadcasted_iota(jnp.int32, (experts, cap), 1)
    live = jnp.where(position < counts[0][:, None], gate_weight[0], jnp.zeros_like(gate_weight[0]))

    def rows(a):
        a = a.reshape(NX, 2, NC, cap).transpose(0, 2, 1, 3).reshape(experts * cap, 1)
        return jnp.broadcast_to(a, (experts * cap, Q)).reshape(experts * cap * Q, 1)

    slot_rows = rows(slots[0])
    dims = (Q, experts * cap * Q, tok_dev)
    pick = (
        (slot_rows[None] == lax.broadcasted_iota(jnp.int32, dims, 2))
        & (lax.broadcasted_iota(jnp.int32, dims, 1) % Q == lax.broadcasted_iota(jnp.int32, dims, 0))
    ).astype(jnp.bfloat16)
    got_in, got_scaled = spread(tokens, cotangent, pick, rows(live))
    flat_in = got_in.reshape(-1, width)
    flat_scaled = got_scaled.reshape(-1, width)
    gate_mat, up_mat, down_mat = w_gate[0], w_up[0], w_down[0]
    pre_gate = jnp.dot(flat_in, gate_mat, preferred_element_type=jnp.float32)
    pre_up = jnp.dot(flat_in, up_mat, preferred_element_type=jnp.float32)
    sigma = jax.nn.sigmoid(pre_gate)
    silu_val = pre_gate * sigma
    act = (silu_val * pre_up).astype(jnp.bfloat16)
    grad_hidden = contract_cols(flat_scaled, down_mat)
    grad_pre_gate = (grad_hidden * pre_up * sigma * (1.0 + pre_gate * (1.0 - sigma))).astype(
        jnp.bfloat16
    )
    grad_pre_up = (grad_hidden * silu_val).astype(jnp.bfloat16)
    acc_gate = contract_rows(flat_in, grad_pre_gate)
    acc_up = contract_rows(flat_in, grad_pre_up)
    acc_down = contract_rows(act, flat_scaled)
    part = contract_cols(grad_pre_gate, gate_mat) + contract_cols(grad_pre_up, up_mat)
    part = part.astype(jnp.bfloat16).reshape(4, NZ, 16, width)
    grad_tokens = collect(part, pick, tok_dev)
    return (
        grad_tokens,
        acc_gate.astype(jnp.bfloat16)[None],
        acc_up.astype(jnp.bfloat16)[None],
        acc_down.astype(jnp.bfloat16)[None],
    )


def solution(mesh):
    in_specs = (
        P(("group", "blk"), None),
        P(("group", "blk"), None),
        P("group", None, "blk"),
        P("group", None, "blk"),
        P("group", "blk", None),
        P(("group", "blk"), None, None),
        P(("group", "blk"), None),
        P(("group", "blk"), None, None),
    )
    out_specs = (
        P(("group", "blk"), None),
        P("group", None, "blk"),
        P("group", None, "blk"),
        P("group", "blk", None),
    )
    return jax.shard_map(body, mesh=mesh, in_specs=in_specs, out_specs=out_specs, check_vma=False)
```

```python
import jax
import jax.numpy as jnp
from jax import lax
from jax.experimental import pallas as pl
from jax.experimental.pallas import tpu as pltpu
from jax.sharding import PartitionSpec as P

MESH = pl.DeviceIdType.MESH
NX, NY, NZ, NC, RUN = 4, 4, 8, 2, 4
Q = 4
HOPS = (0, 1, 7, 2, 6, 3, 5, 4)


def contract_rows(left, right):
    return lax.dot_general(
        left, right, (((0,), (0,)), ((), ())), preferred_element_type=jnp.float32
    )


def contract_cols(left, right):
    return lax.dot_general(
        left, right, (((1,), (1,)), ((), ())), preferred_element_type=jnp.float32
    )


def place():
    group, blk = lax.axis_index("group"), lax.axis_index("blk")
    x, z_hi, core = group // 4, (group // 2) % 2, group % 2
    y, z_lo = blk // RUN, blk % RUN
    return x, y, z_hi * RUN + z_lo, core


def device(x, y, z, core):
    return (x * 4 + (z // RUN) * 2 + core, y * RUN + z % RUN)


def x_peers(me):
    x, y, z, core = me
    for step in range(1, NX * NC):
        px, pc = (x + step // NC) % NX, (core + step % NC) % NC
        yield step - 1, px * NC + pc, device(px, y, z, pc)


def greet(me):
    x, y, z, core = me
    barrier = pltpu.get_barrier_semaphore()
    peers = [d for _, _, d in x_peers(me)]
    peers += [device(x, y, (z + hop) % NZ, core) for hop in range(1, NZ)]
    peers += [device(x, (y + 1) % NY, z, core), device(x, (y + 3) % NY, z, core)]
    for peer in peers:
        pl.semaphore_signal(barrier, inc=1, device_id=peer, device_id_type=MESH)
    pl.semaphore_wait(barrier, len(peers))


def remote(src, dst, send, recv, to):
    return pltpu.make_async_remote_copy(
        src_ref=src, dst_ref=dst, send_sem=send, recv_sem=recv, device_id=to, device_id_type=MESH
    )


def order_matrix():
    row = lax.broadcasted_iota(jnp.int32, (128, 128), 0)
    col = lax.broadcasted_iota(jnp.int32, (128, 128), 1)
    h, q, s, c = row // 64, (row // 16) % 4, (row // 2) % 8, row % 2
    return (col == s * 16 + h * 8 + c * 4 + q).astype(jnp.bfloat16)


def kernel(
    tok_hbm, cot_hbm, gate_hbm, up_hbm, down_hbm, pick_ref, scale_ref,
    out_ref, gate_out, up_out, down_out,
    given, both, w_down, mess, recv, block, rows_in, rows_sc, pre, grad_hid, grads, act,
    part, half_in, side_in, z_in, back, back_in, g_gate, g_up, g_down,
    load_sem, own_sem, store_sem,
    xs, xr, zs, zr, ys, yr, fs, fr, hs, hr, ds, dr, ss, sr, bs, br, cs, cr,
):
    f32, bf = jnp.float32, jnp.bfloat16
    me = place()
    x, y, z, core = me
    mine = x * NC + core
    dim = given.shape[-1]
    width, half = dim // Q, dim // 2
    hid = w_down.shape[0]
    rows = (rows_in, rows_sc)
    order = order_matrix()
    up, down = device(x, (y + 1) % NY, z, core), device(x, (y + 3) % NY, z, core)
    cols = (pl.ds(0, half), pl.ds(half, half))

    loads = [
        pltpu.make_async_copy(src, dst, load_sem.at[i])
        for i, (src, dst) in enumerate((
            (tok_hbm, given.at[0]), (cot_hbm, given.at[1]),
            (gate_hbm, both.at[:, pl.ds(0, hid)]), (up_hbm, both.at[:, pl.ds(hid, hid)]),
            (down_hbm, w_down),
        ))
    ]
    for load in loads:
        load.start()
    greet(me)

    def x_copy(t, i, slot, to):
        return remote(mess.at[t, slot], recv.at[t, mine], xs.at[t, i], xr.at[t, i], to)

    for t in range(2):
        loads[t].wait()
        total = jnp.zeros((128, width), f32)
        for q in range(Q):
            total = total + jnp.dot(
                pick_ref[q], given[t, :, q * width:(q + 1) * width], preferred_element_type=f32
            )
        if t == 1:
            total = total * scale_ref[...]
        mess[t] = total.astype(bf).reshape(8, 16, width)
        for i, slot, to in x_peers(me):
            x_copy(t, i, slot, to).start()
        recv[t, pl.ds(mine, 1)] = mess[t, pl.ds(mine, 1)]

    def at(ref, j, k, *more):
        return ref.at[(k // 4, j, k % 4) + more]

    def z_copy(t, k):
        zt = (z + HOPS[k]) % NZ
        return remote(
            block.at[t, zt // RUN], at(rows[t], 0, k), zs.at[t, k], zr.at[t, k],
            device(x, y, zt, core),
        )

    def y_copy(t, k, side):
        src = at(rows[t], 0, k) if k else block.at[t, z // RUN]
        return remote(
            src, at(rows[t], 1 + side, k), ys.at[t, side, k], yr.at[t, side, k],
            down if side else up,
        )

    def f_copy(t, k, side):
        c = (slice(None), cols[side])
        return remote(
            at(rows[t], 1 + side, k, *c), at(rows[t], 3, k, *c),
            fs.at[t, side, k], fr.at[t, side, k], down if side else up,
        )

    def own_copy(t):
        return pltpu.make_async_copy(block.at[t, z // RUN], at(rows[t], 0, 0), own_sem.at[t])

    for t in range(2):
        for i, slot, to in x_peers(me):
            x_copy(t, i, slot, to).wait_recv()
        moved = jnp.dot(
            order, recv[t].reshape(128, width), preferred_element_type=f32
        ).astype(bf)
        for h in range(2):
            for q in range(Q):
                start = (h * Q + q) * 16
                block[t, h, :, q * width:(q + 1) * width] = moved[start:start + 16]
        for side in range(2):
            y_copy(t, 0, side).start()
        for k in range(1, 4):
            z_copy(t, k).start()
        own_copy(t).start()
    for t in range(2):
        for k in range(4, NZ):
            z_copy(t, k).start()

    def arrived(t, hf):
        if hf == 0:
            own_copy(t).wait()
        for k in range(4 * hf, 4 * hf + 4):
            for side in range(2):
                f_copy(t, k, side).wait_recv()

    def chunk(c, size):
        return pl.ds(pl.multiple_of(c * size, size), size)

    def pre_acts(hf):
        pre[...] = jnp.zeros_like(pre)

        @pl.loop(0, dim // 1024)
        def _(c):
            cc = chunk(c, 1024)
            pre[...] += jnp.dot(
                rows_in[hf, :, :, :, cc].reshape(256, 1024), both[cc, :], preferred_element_type=f32
            )

    def hidden(hf):
        grad_hid[...] = jnp.zeros_like(grad_hid)

        @pl.loop(0, dim // 1024)
        def _(c):
            cc = chunk(c, 1024)
            grad_hid[...] += contract_cols(
                rows_sc[hf, :, :, :, cc].reshape(256, 1024), w_down[:, cc]
            )

        gate, lift, grad = pre[:, :hid], pre[:, hid:], grad_hid[...]
        sigma = jax.nn.sigmoid(gate)
        silu = gate * sigma
        act[hf] = (silu * lift).astype(bf)
        grads[hf, :, :hid] = (grad * lift * sigma * (1.0 + gate * (1.0 - sigma))).astype(bf)
        grads[hf, :, hid:] = (grad * silu).astype(bf)

    def parts(hf, lo, hi):
        @pl.loop(lo, hi)
        def _(c):
            cc = chunk(c, 512)
            part[hf, :, :, :, cc] = contract_cols(grads[hf], both[cc, :]).astype(bf).reshape(
                4, 4, 16, 512
            )

    def forward(t, k):
        for side in range(2):
            y_copy(t, k, side).wait_recv()
            f_copy(t, k, side).start()

    units = [(t, k) for hf in range(2) for t in range(2) for k in range(4 * hf, 4 * hf + 4)]
    for load in loads[2:]:
        load.wait()
    for i, (t, k) in enumerate(units):
        if k:
            z_copy(t, k).wait_recv()
            for side in range(2):
                y_copy(t, k, side).start()
        if i:
            forward(*units[i - 1])
        if i == 9:
            arrived(0, 0)
            pre_acts(0)
        if i == 11:
            arrived(1, 0)
            hidden(0)
        if i == 12:
            parts(0, 0, 7)
        if i == 13:
            parts(0, 7, 14)
    forward(*units[-1])

    sides = (down, up)

    def h_copy(k, side):
        return remote(
            at(part, 3, k, slice(None), cols[side]), half_in.at[side, k],
            hs.at[side, k], hr.at[side, k], sides[side],
        )

    def d_copy(k, side):
        return remote(
            at(part, 1 + side, k, slice(None), cols[1 - side]), side_in.at[side, k, :, cols[1 - side]],
            ds.at[side, k], dr.at[side, k], sides[side],
        )

    def s_copy(k, side):
        return remote(
            at(part, 1 + side, k, slice(None), cols[side]), side_in.at[side, k, :, cols[side]],
            ss.at[side, k], sr.at[side, k], sides[side],
        )

    def b_copy(k):
        zt = (z + NZ - HOPS[k]) % NZ
        return remote(at(part, 0, k), z_in.at[z], bs.at[k], br.at[k], device(x, y, zt, core))

    def first(k):
        for side in range(2):
            h_copy(k, side).start()

    def direct(k):
        for side in range(2):
            d_copy(k, side).start()

    def relay(k):
        for side in range(2):
            h_copy(k, side).wait_recv()
            own = part[k // 4, 1 + side, k % 4, :, cols[side]]
            part[k // 4, 1 + side, k % 4, :, cols[side]] = (
                half_in[side, k].astype(f32) + own.astype(f32)
            ).astype(bf)
            s_copy(k, side).start()

    def finish(k):
        for side in range(2):
            d_copy(k, side).wait_recv()
            s_copy(k, side).wait_recv()
        total = (
            part[k // 4, 0, k % 4].astype(f32) + side_in[0, k].astype(f32) + side_in[1, k].astype(f32)
        ).astype(bf)
        if k:
            part[k // 4, 0, k % 4] = total
            b_copy(k).start()
        else:
            z_in[pl.ds(z, 1)] = total[None]

    def weights_in(lo, hi):
        @pl.loop(lo, hi)
        def _(c):
            cc = chunk(c, 512)
            got = contract_rows(
                rows_in[:, :, :, :, cc].reshape(512, 512), grads[...].reshape(512, 2 * hid)
            ).astype(bf)
            g_gate[cc, :] = got[:, :hid]
            g_up[cc, :] = got[:, hid:]

    def weights_down(lo, hi):
        @pl.loop(lo, hi)
        def _(c):
            cc = chunk(c, 512)
            g_down[:, cc] = contract_rows(
                act[...].reshape(512, hid), rows_sc[:, :, :, :, cc].reshape(512, 512)
            ).astype(bf)

    stores = [
        pltpu.make_async_copy(src, dst, store_sem.at[i])
        for i, (src, dst) in enumerate(((g_gate, gate_out), (g_up, up_out), (g_down, down_out)))
    ]

    for k in (3, 2, 1, 0):
        first(k)
        direct(k)
    arrived(0, 1)
    pre_acts(1)
    arrived(1, 1)
    hidden(1)
    parts(1, 0, 14)
    for k in (3, 2, 1, 0):
        relay(k)
    for k in (7, 6, 5, 4):
        first(k)
        direct(k)
    weights_in(0, 7)
    for k in (3, 2):
        finish(k)
    weights_in(7, 14)
    for store in stores[:2]:
        store.start()
    for k in (1, 0):
        finish(k)
    for k in (7, 6, 5, 4):
        relay(k)
    weights_down(0, 14)
    stores[2].start()
    for k in (7, 6, 5, 4):
        finish(k)

    for k in range(1, NZ):
        b_copy(k).wait_recv()
    pieces = []
    for h in range(2):
        for q in range(Q):
            c = slice(q * width, (q + 1) * width)
            acc = z_in[h * RUN, :, c].astype(f32)
            for l in range(1, RUN):
                acc = acc + z_in[h * RUN + l, :, c].astype(f32)
            pieces.append(acc.astype(bf))
    back[...] = contract_rows(order, jnp.concatenate(pieces, axis=0)).astype(bf).reshape(8, 16, width)

    def c_copy(i, slot, to):
        return remote(back.at[slot], back_in.at[mine], cs.at[i], cr.at[i], to)

    for i, slot, to in x_peers(me):
        c_copy(i, slot, to).start()
    back_in[pl.ds(mine, 1)] = back[pl.ds(mine, 1)]
    for i, slot, to in x_peers(me):
        c_copy(i, slot, to).wait_recv()
    for q in range(Q):
        out_ref[:, q * width:(q + 1) * width] = contract_rows(
            pick_ref[q], back_in[...].reshape(128, width)
        ).astype(bf)

    for i, slot, to in x_peers(me):
        for t in range(2):
            x_copy(t, i, slot, to).wait_send()
        c_copy(i, slot, to).wait_send()
    for k in range(NZ):
        for side in range(2):
            for t in range(2):
                y_copy(t, k, side).wait_send()
                f_copy(t, k, side).wait_send()
            h_copy(k, side).wait_send()
            d_copy(k, side).wait_send()
            s_copy(k, side).wait_send()
        if k:
            for t in range(2):
                z_copy(t, k).wait_send()
            b_copy(k).wait_send()
    for store in stores:
        store.wait()


def experts_backward(tokens, cotangent, w_gate, w_up, w_down, pick, scale):
    dim, hid = w_gate.shape
    bf, f32 = jnp.bfloat16, jnp.float32
    vmem, hbm = pl.BlockSpec(memory_space=pltpu.VMEM), pl.BlockSpec(memory_space=pl.ANY)
    dma = pltpu.SemaphoreType.DMA
    message = pltpu.VMEM((8, 16, dim // Q), bf)
    side = dma((2, NZ))
    two_sides = dma((2, 2, NZ))
    return pl.pallas_call(
        kernel,
        out_shape=(
            jax.ShapeDtypeStruct(tokens.shape, bf),
            jax.ShapeDtypeStruct((dim, hid), bf),
            jax.ShapeDtypeStruct((dim, hid), bf),
            jax.ShapeDtypeStruct((hid, dim), bf),
        ),
        in_specs=[hbm] * 5 + [vmem] * 2,
        out_specs=(vmem, hbm, hbm, hbm),
        scratch_shapes=[
            pltpu.VMEM((2,) + tokens.shape, bf),
            pltpu.VMEM((dim, 2 * hid), bf),
            pltpu.VMEM((hid, dim), bf),
            pltpu.VMEM((2, 8, 16, dim // Q), bf),
            pltpu.VMEM((2, 8, 16, dim // Q), bf),
            pltpu.VMEM((2, 2, 16, dim), bf),
            pltpu.VMEM((2, 4, 4, 16, dim), bf),
            pltpu.VMEM((2, 4, 4, 16, dim), bf),
            pltpu.VMEM((256, 2 * hid), f32),
            pltpu.VMEM((256, hid), f32),
            pltpu.VMEM((2, 256, 2 * hid), bf),
            pltpu.VMEM((2, 256, hid), bf),
            pltpu.VMEM((2, 4, 4, 16, dim), bf),
            pltpu.VMEM((2, NZ, 16, dim // 2), bf),
            pltpu.VMEM((2, NZ, 16, dim), bf),
            pltpu.VMEM((NZ, 16, dim), bf),
            message, message,
            pltpu.VMEM((dim, hid), bf),
            pltpu.VMEM((dim, hid), bf),
            pltpu.VMEM((hid, dim), bf),
            dma((5,)), dma((2,)), dma((3,)),
            dma((2, 7)), dma((2, 7)), side, side,
            two_sides, two_sides, two_sides, two_sides,
            side, side, side, side, side, side,
            dma((NZ,)), dma((NZ,)), dma((7,)), dma((7,)),
        ],
        compiler_params=pltpu.CompilerParams(
            collective_id=0, has_side_effects=True, vmem_limit_bytes=62 * 2**20
        ),
        name="experts_backward",
    )(tokens, cotangent, w_gate, w_up, w_down, pick, scale)


def body(tokens, cotangent, w_gate, w_up, w_down, gate_weight, counts, slots):
    experts = counts.shape[1]
    cap = slots.shape[2]
    tok_dev = tokens.shape[0]
    position = lax.broadcasted_iota(jnp.int32, (experts, cap), 1)
    live = jnp.where(position < counts[0][:, None], gate_weight[0], jnp.zeros_like(gate_weight[0]))

    def rows(a):
        a = a.reshape(NX, 2, NC, cap).transpose(0, 2, 1, 3).reshape(experts * cap, 1)
        return jnp.broadcast_to(a, (experts * cap, Q)).reshape(experts * cap * Q, 1)

    slot_rows = rows(slots[0])
    dims = (Q, experts * cap * Q, tok_dev)
    pick = (
        (slot_rows[None] == lax.broadcasted_iota(jnp.int32, dims, 2))
        & (lax.broadcasted_iota(jnp.int32, dims, 1) % Q == lax.broadcasted_iota(jnp.int32, dims, 0))
    ).astype(jnp.bfloat16)
    grad_tokens, grad_gate, grad_up, grad_down = experts_backward(
        tokens, cotangent, w_gate[0], w_up[0], w_down[0], pick, rows(live)
    )
    return grad_tokens, grad_gate[None], grad_up[None], grad_down[None]


def solution(mesh):
    in_specs = (
        P(("group", "blk"), None),
        P(("group", "blk"), None),
        P("group", None, "blk"),
        P("group", None, "blk"),
        P("group", "blk", None),
        P(("group", "blk"), None, None),
        P(("group", "blk"), None),
        P(("group", "blk"), None, None),
    )
    out_specs = (
        P(("group", "blk"), None),
        P("group", None, "blk"),
        P("group", None, "blk"),
        P("group", "blk", None),
    )
    return jax.shard_map(body, mesh=mesh, in_specs=in_specs, out_specs=out_specs, check_vma=False)
```

```python
import jax
import jax.numpy as jnp
from jax import lax
from jax.experimental import pallas as pl
from jax.experimental.pallas import tpu as pltpu
from jax.sharding import PartitionSpec as P

MESH = pl.DeviceIdType.MESH
NX, NY, NZ, NC, RUN = 4, 4, 8, 2, 4
Q = 4
HOPS = (0, 1, 5, 4, 7, 2, 6, 3)


def contract_rows(left, right):
    return lax.dot_general(
        left, right, (((0,), (0,)), ((), ())), preferred_element_type=jnp.float32
    )


def contract_cols(left, right):
    return lax.dot_general(
        left, right, (((1,), (1,)), ((), ())), preferred_element_type=jnp.float32
    )


def place():
    group, blk = lax.axis_index("group"), lax.axis_index("blk")
    x, z_hi, core = group // 4, (group // 2) % 2, group % 2
    y, z_lo = blk // RUN, blk % RUN
    return x, y, z_hi * RUN + z_lo, core


def device(x, y, z, core):
    return (x * 4 + (z // RUN) * 2 + core, y * RUN + z % RUN)


def x_peers(me):
    x, y, z, core = me
    for step in range(1, NX * NC):
        px, pc = (x + step // NC) % NX, (core + step % NC) % NC
        yield step - 1, px * NC + pc, device(px, y, z, pc)


def greet(me):
    x, y, z, core = me
    barrier = pltpu.get_barrier_semaphore()
    peers = [d for _, _, d in x_peers(me)]
    peers += [device(x, y, (z + hop) % NZ, core) for hop in range(1, NZ)]
    peers += [device(x, (y + 1) % NY, z, core), device(x, (y + 3) % NY, z, core)]
    for peer in peers:
        pl.semaphore_signal(barrier, inc=1, device_id=peer, device_id_type=MESH)
    pl.semaphore_wait(barrier, len(peers))


def remote(src, dst, send, recv, to):
    return pltpu.make_async_remote_copy(
        src_ref=src, dst_ref=dst, send_sem=send, recv_sem=recv, device_id=to, device_id_type=MESH
    )


def order_matrix():
    row = lax.broadcasted_iota(jnp.int32, (128, 128), 0)
    col = lax.broadcasted_iota(jnp.int32, (128, 128), 1)
    h, q, s, c = row // 64, (row // 16) % 4, (row // 2) % 8, row % 2
    return (col == s * 16 + h * 8 + c * 4 + q).astype(jnp.bfloat16)


def kernel(
    tok_hbm, cot_hbm, gate_hbm, up_hbm, down_hbm, weight_ref, count_ref, slot_ref,
    out_ref, g_gate, g_up, g_down,
    given, both, w_down, mess, recv, block, rows_in, rows_sc, pre, grad_hid, grads, act,
    part, half_in, side_in, z_in, back, back_in, pick_ref,
    load_sem, own_sem,
    xs, xr, zs, zr, ys, yr, fs, fr, hs, hr, ds, dr, ss, sr, bs, br, cs, cr,
):
    f32, bf = jnp.float32, jnp.bfloat16
    me = place()
    x, y, z, core = me
    mine = x * NC + core
    dim = given.shape[-1]
    width, half = dim // Q, dim // 2
    hid = w_down.shape[0]
    rows = (rows_in, rows_sc)
    order = order_matrix()
    up, down = device(x, (y + 1) % NY, z, core), device(x, (y + 3) % NY, z, core)
    cols = (pl.ds(0, half), pl.ds(half, half))

    loads = [
        pltpu.make_async_copy(src, dst, load_sem.at[i])
        for i, (src, dst) in enumerate((
            (tok_hbm, given.at[0]), (cot_hbm, given.at[1]),
            (gate_hbm, both.at[:, pl.ds(0, hid)]), (up_hbm, both.at[:, pl.ds(hid, hid)]),
            (down_hbm, w_down),
        ))
    ]
    for load in loads:
        load.start()
    greet(me)

    shape = (128, slot_ref.shape[1])
    row = lax.broadcasted_iota(jnp.int32, shape, 0)
    here = lax.broadcasted_iota(jnp.int32, shape, 1) == (
        row // 32 * 4 + row // 8 % 2 * 2 + row // 16 % 2
    )
    second = row // 4 % 2 == 1

    def of_row(table):
        value = jnp.where(second, table[1:2], table[0:1])
        return jnp.sum(jnp.where(here, value, jnp.zeros_like(value)), axis=1, keepdims=True)

    position = lax.broadcasted_iota(jnp.int32, weight_ref.shape, 0)
    scale = of_row(
        jnp.where(position < count_ref[...], weight_ref[...], jnp.zeros_like(weight_ref[...]))
    )
    slot_row = of_row(slot_ref[...].astype(f32))
    spots = (128, given.shape[1])
    wanted = slot_row == lax.broadcasted_iota(jnp.int32, spots, 1).astype(f32)
    part_of_row = lax.broadcasted_iota(jnp.int32, spots, 0) % Q
    for q in range(Q):
        pick_ref[q] = (wanted & (part_of_row == q)).astype(f32).astype(bf)

    def x_copy(t, i, slot, to):
        return remote(mess.at[t, slot], recv.at[t, mine], xs.at[t, i], xr.at[t, i], to)

    for t in range(2):
        loads[t].wait()
        total = jnp.zeros((128, width), f32)
        for q in range(Q):
            total = total + jnp.dot(
                pick_ref[q], given[t, :, q * width:(q + 1) * width], preferred_element_type=f32
            )
        if t == 1:
            total = total * scale
        mess[t] = total.astype(bf).reshape(8, 16, width)
        for i, slot, to in x_peers(me):
            x_copy(t, i, slot, to).start()
        recv[t, pl.ds(mine, 1)] = mess[t, pl.ds(mine, 1)]

    def at(ref, j, k, *more):
        return ref.at[(k // 4, j, k % 4) + more]

    def z_copy(t, k):
        zt = (z + HOPS[k]) % NZ
        return remote(
            block.at[t, zt // RUN], at(rows[t], 0, k), zs.at[t, k], zr.at[t, k],
            device(x, y, zt, core),
        )

    def y_copy(t, k, side):
        src = at(rows[t], 0, k) if k else block.at[t, z // RUN]
        return remote(
            src, at(rows[t], 1 + side, k), ys.at[t, side, k], yr.at[t, side, k],
            down if side else up,
        )

    def f_copy(t, k, side):
        c = (slice(None), cols[side])
        return remote(
            at(rows[t], 1 + side, k, *c), at(rows[t], 3, k, *c),
            fs.at[t, side, k], fr.at[t, side, k], down if side else up,
        )

    def own_copy(t):
        return pltpu.make_async_copy(block.at[t, z // RUN], at(rows[t], 0, 0), own_sem.at[t])

    for t in range(2):
        for i, slot, to in x_peers(me):
            x_copy(t, i, slot, to).wait_recv()
        moved = jnp.dot(
            order, recv[t].reshape(128, width), preferred_element_type=f32
        ).astype(bf)
        for h in range(2):
            for q in range(Q):
                start = (h * Q + q) * 16
                block[t, h, :, q * width:(q + 1) * width] = moved[start:start + 16]
        for side in range(2):
            y_copy(t, 0, side).start()
        for k in range(1, 4):
            z_copy(t, k).start()
        own_copy(t).start()
    for t in range(2):
        for k in range(4, NZ):
            z_copy(t, k).start()

    def arrived(t, hf):
        if hf == 0:
            own_copy(t).wait()
        for k in range(4 * hf, 4 * hf + 4):
            for side in range(2):
                f_copy(t, k, side).wait_recv()

    def chunk(c, size):
        return pl.ds(pl.multiple_of(c * size, size), size)

    def pre_acts(hf):
        pre[...] = jnp.zeros_like(pre)

        @pl.loop(0, dim // 1024)
        def _(c):
            cc = chunk(c, 1024)
            pre[...] += jnp.dot(
                rows_in[hf, :, :, :, cc].reshape(256, 1024), both[cc, :], preferred_element_type=f32
            )

    def hidden(hf):
        grad_hid[...] = jnp.zeros_like(grad_hid)

        @pl.loop(0, dim // 1024)
        def _(c):
            cc = chunk(c, 1024)
            grad_hid[...] += contract_cols(
                rows_sc[hf, :, :, :, cc].reshape(256, 1024), w_down[:, cc]
            )

        gate, lift, grad = pre[:, :hid], pre[:, hid:], grad_hid[...]
        sigma = jax.nn.sigmoid(gate)
        silu = gate * sigma
        act[hf] = (silu * lift).astype(bf)
        grads[hf, :, :hid] = (grad * lift * sigma * (1.0 + gate * (1.0 - sigma))).astype(bf)
        grads[hf, :, hid:] = (grad * silu).astype(bf)

    def parts(hf, lo, hi):
        @pl.loop(lo, hi)
        def _(c):
            cc = chunk(c, 512)
            part[hf, :, :, :, cc] = contract_cols(grads[hf], both[cc, :]).astype(bf).reshape(
                4, 4, 16, 512
            )

    def forward(t, k):
        for side in range(2):
            y_copy(t, k, side).wait_recv()
            f_copy(t, k, side).start()

    units = [(t, k) for hf in range(2) for t in range(2) for k in range(4 * hf, 4 * hf + 4)]
    for load in loads[2:]:
        load.wait()
    for i, (t, k) in enumerate(units):
        if k:
            z_copy(t, k).wait_recv()
            for side in range(2):
                y_copy(t, k, side).start()
        if i:
            forward(*units[i - 1])
        if i == 9:
            arrived(0, 0)
            pre_acts(0)
        if i == 11:
            arrived(1, 0)
            hidden(0)
        if i == 12:
            parts(0, 0, 7)
        if i == 13:
            parts(0, 7, 14)
    forward(*units[-1])

    sides = (down, up)

    def h_copy(k, side):
        return remote(
            at(part, 3, k, slice(None), cols[side]), half_in.at[side, k],
            hs.at[side, k], hr.at[side, k], sides[side],
        )

    def d_copy(k, side):
        return remote(
            at(part, 1 + side, k, slice(None), cols[1 - side]), side_in.at[side, k, :, cols[1 - side]],
            ds.at[side, k], dr.at[side, k], sides[side],
        )

    def s_copy(k, side):
        return remote(
            at(part, 1 + side, k, slice(None), cols[side]), side_in.at[side, k, :, cols[side]],
            ss.at[side, k], sr.at[side, k], sides[side],
        )

    def b_copy(k):
        zt = (z + NZ - HOPS[k]) % NZ
        return remote(at(part, 0, k), z_in.at[z], bs.at[k], br.at[k], device(x, y, zt, core))

    def first(k):
        for side in range(2):
            h_copy(k, side).start()

    def direct(k):
        for side in range(2):
            d_copy(k, side).start()

    def relay(k):
        for side in range(2):
            h_copy(k, side).wait_recv()
            own = part[k // 4, 1 + side, k % 4, :, cols[side]]
            part[k // 4, 1 + side, k % 4, :, cols[side]] = (
                half_in[side, k].astype(f32) + own.astype(f32)
            ).astype(bf)
            s_copy(k, side).start()

    def finish(k):
        for side in range(2):
            d_copy(k, side).wait_recv()
            s_copy(k, side).wait_recv()
        total = (
            part[k // 4, 0, k % 4].astype(f32) + side_in[0, k].astype(f32) + side_in[1, k].astype(f32)
        ).astype(bf)
        if k:
            part[k // 4, 0, k % 4] = total
            b_copy(k).start()
        else:
            z_in[pl.ds(z, 1)] = total[None]

    def weights_in(lo, hi):
        @pl.loop(lo, hi)
        def _(c):
            cc = chunk(c, 512)
            got = contract_rows(
                rows_in[:, :, :, :, cc].reshape(512, 512), grads[...].reshape(512, 2 * hid)
            ).astype(bf)
            g_gate[cc, :] = got[:, :hid]
            g_up[cc, :] = got[:, hid:]

    def weights_down(lo, hi):
        @pl.loop(lo, hi)
        def _(c):
            cc = chunk(c, 512)
            g_down[:, cc] = contract_rows(
                act[...].reshape(512, hid), rows_sc[:, :, :, :, cc].reshape(512, 512)
            ).astype(bf)

    for k in (3, 2, 1, 0):
        first(k)
        direct(k)
    arrived(0, 1)
    pre_acts(1)
    arrived(1, 1)
    hidden(1)
    parts(1, 0, 14)
    relay(3)
    relay(2)
    first(7)
    relay(1)
    relay(0)
    first(6)
    direct(7)
    weights_in(0, 2)
    finish(3)
    finish(2)
    relay(7)
    first(5)
    direct(6)
    weights_in(2, 5)
    finish(1)
    finish(0)
    relay(6)
    first(4)
    direct(5)
    weights_in(5, 8)
    finish(7)
    relay(5)
    direct(4)
    weights_in(8, 11)
    finish(6)
    relay(4)
    weights_in(11, 14)
    finish(5)
    weights_down(0, 14)
    finish(4)

    for k in range(1, NZ):
        b_copy(k).wait_recv()
    pieces = []
    for h in range(2):
        for q in range(Q):
            c = slice(q * width, (q + 1) * width)
            acc = z_in[h * RUN, :, c].astype(f32)
            for l in range(1, RUN):
                acc = acc + z_in[h * RUN + l, :, c].astype(f32)
            pieces.append(acc.astype(bf))
    back[...] = contract_rows(order, jnp.concatenate(pieces, axis=0)).astype(bf).reshape(8, 16, width)

    def c_copy(i, slot, to):
        return remote(back.at[slot], back_in.at[mine], cs.at[i], cr.at[i], to)

    for i, slot, to in x_peers(me):
        c_copy(i, slot, to).start()
    back_in[pl.ds(mine, 1)] = back[pl.ds(mine, 1)]
    for i, slot, to in x_peers(me):
        c_copy(i, slot, to).wait_recv()
    for q in range(Q):
        out_ref[:, q * width:(q + 1) * width] = contract_rows(
            pick_ref[q], back_in[...].reshape(128, width)
        ).astype(bf)

    for i, slot, to in x_peers(me):
        for t in range(2):
            x_copy(t, i, slot, to).wait_send()
        c_copy(i, slot, to).wait_send()
    for k in range(NZ):
        for side in range(2):
            for t in range(2):
                y_copy(t, k, side).wait_send()
                f_copy(t, k, side).wait_send()
            h_copy(k, side).wait_send()
            d_copy(k, side).wait_send()
            s_copy(k, side).wait_send()
        if k:
            for t in range(2):
                z_copy(t, k).wait_send()
            b_copy(k).wait_send()


def experts_backward(tokens, cotangent, w_gate, w_up, w_down, weight, count, slot):
    dim, hid = w_gate.shape
    bf, f32 = jnp.bfloat16, jnp.float32
    vmem, hbm = pl.BlockSpec(memory_space=pltpu.VMEM), pl.BlockSpec(memory_space=pltpu.HBM)
    dma = pltpu.SemaphoreType.DMA
    message = pltpu.VMEM((8, 16, dim // Q), bf)
    side = dma((2, NZ))
    two_sides = dma((2, 2, NZ))
    return pl.pallas_call(
        kernel,
        out_shape=(
            jax.ShapeDtypeStruct(tokens.shape, bf),
            jax.ShapeDtypeStruct((dim, hid), bf),
            jax.ShapeDtypeStruct((dim, hid), bf),
            jax.ShapeDtypeStruct((hid, dim), bf),
        ),
        in_specs=[hbm] * 5 + [vmem] * 3,
        out_specs=(vmem,) * 4,
        scratch_shapes=[
            pltpu.VMEM((2,) + tokens.shape, bf),
            pltpu.VMEM((dim, 2 * hid), bf),
            pltpu.VMEM((hid, dim), bf),
            pltpu.VMEM((2, 8, 16, dim // Q), bf),
            pltpu.VMEM((2, 8, 16, dim // Q), bf),
            pltpu.VMEM((2, 2, 16, dim), bf),
            pltpu.VMEM((2, 4, 4, 16, dim), bf),
            pltpu.VMEM((2, 4, 4, 16, dim), bf),
            pltpu.VMEM((256, 2 * hid), f32),
            pltpu.VMEM((256, hid), f32),
            pltpu.VMEM((2, 256, 2 * hid), bf),
            pltpu.VMEM((2, 256, hid), bf),
            pltpu.VMEM((2, 4, 4, 16, dim), bf),
            pltpu.VMEM((2, NZ, 16, dim // 2), bf),
            pltpu.VMEM((2, NZ, 16, dim), bf),
            pltpu.VMEM((NZ, 16, dim), bf),
            message, message,
            pltpu.VMEM((Q, 128, tokens.shape[0]), bf),
            dma((5,)), dma((2,)),
            dma((2, 7)), dma((2, 7)), side, side,
            two_sides, two_sides, two_sides, two_sides,
            side, side, side, side, side, side,
            dma((NZ,)), dma((NZ,)), dma((7,)), dma((7,)),
        ],
        compiler_params=pltpu.CompilerParams(
            collective_id=0, has_side_effects=True, vmem_limit_bytes=45 * 2**20
        ),
        name="experts_backward",
    )(tokens, cotangent, w_gate, w_up, w_down, weight, count, slot)


def body(tokens, cotangent, w_gate, w_up, w_down, gate_weight, counts, slots):
    grad_tokens, grad_gate, grad_up, grad_down = experts_backward(
        tokens, cotangent, w_gate[0], w_up[0], w_down[0], gate_weight[0].T, counts, slots[0].T
    )
    return grad_tokens, grad_gate[None], grad_up[None], grad_down[None]


def solution(mesh):
    in_specs = (
        P(("group", "blk"), None),
        P(("group", "blk"), None),
        P("group", None, "blk"),
        P("group", None, "blk"),
        P("group", "blk", None),
        P(("group", "blk"), None, None),
        P(("group", "blk"), None),
        P(("group", "blk"), None, None),
    )
    out_specs = (
        P(("group", "blk"), None),
        P("group", None, "blk"),
        P("group", None, "blk"),
        P("group", "blk", None),
    )
    return jax.shard_map(body, mesh=mesh, in_specs=in_specs, out_specs=out_specs, check_vma=False)
```
